128 devices in a mesh: seq: 2 (over core), chan: 64 (over z, y, x).
Axes of the slice: x: 4, y: 4, z: 4, core: 2. Of those that a mesh axis runs over, the one named last changes fastest.
Arguments:
- tokens: bfloat16 [256, 8192], P('seq', 'chan'), may hold values from -6 to 6
- projection_weights: bfloat16 [3, 8192, 8192], P(None, 'seq', 'chan'), may hold values from -0.0625 to 0.0625
- short_taps: float32 [3, 3, 8192], P(None, None, 'chan'), may hold values from -3.5 to 3.5
- filter_spectra: float32 [2, 512, 8192], P(None, 'seq', 'chan'), may hold values from -8 to 8
Outputs:
- mixed: bfloat16 [256, 8192], P('seq', 'chan')
The draws below stay inside these ranges and needn't reach their ends.
All inputs are finite; a program needn't handle non-finite values.
Results may differ from the reference program's by a relative error of at most 0.0064.
Values may be sent and summed in bfloat16 or wider, within the bound.
No kernel may reach another device: no remote copies, remote signals or barrier semaphores. Data moves between devices by JAX's collectives and lax.ppermute only.
A program may use at most 64 MiB of HBM per device.

```python
import jax
import jax.numpy as jnp
from jax import lax

D = 8192
SHORT = 3
L = 256
FFT_LEN = 512


def shard_levels(rng, shape, split, least, high):
    level, own = 1.0, jax.random.fold_in(rng, 6)
    for position, shards_of in split:
        heights = jnp.exp(jax.random.uniform(jax.random.fold_in(own, position), (shards_of,), jnp.float32, least / len(split), high / len(split)))
        level = level * jnp.repeat(heights, shape[position] // shards_of).reshape([-1 if axis == position else 1 for axis in range(len(shape))])
    return level


def bell_draw(rng, dims, spread, limit, shards=(), held_as=jnp.bfloat16):
    gain = shard_levels(rng, dims, shards, -0.22, 0.18) if shards else 1.0
    values = jax.random.normal(rng, dims, jnp.float32) * spread * gain
    return jnp.minimum(jnp.maximum(values, -limit), limit).astype(held_as)


def setup_inputs(seed: int = 0) -> dict:
    keys = jax.random.split(jax.random.key(seed), 5)
    return {
        "tokens": bell_draw(keys[0], (L, D), 1.0, 6.0, ((0, 2), (1, 64))),
        "projection_weights": bell_draw(keys[1], (3, D, D), D ** -0.5, 0.0625, ((1, 2), (2, 64))),
        "short_taps": bell_draw(keys[2], (3, SHORT, D), SHORT ** -0.5, 3.5, ((2, 64),), jnp.float32),
        "filter_spectra": bell_draw(keys[3], (2, FFT_LEN, D), 1.4, 8.0, ((1, 2), (2, 64)), jnp.float32),
    }


def short_filter(signal_input, kernel_taps):
    width = kernel_taps.shape[0]
    padded = jnp.pad(signal_input, ((width - 1, 0), (0, 0)))
    kernel = kernel_taps[::-1][:, None, :]
    result = lax.conv_general_dilated(padded[None], kernel, (1,), "VALID", dimension_numbers=("NWC", "WIO", "NWC"), feature_group_count=signal_input.shape[1], precision=lax.Precision.HIGHEST)
    return result[0]


def reference(tokens, projection_weights, short_taps, filter_spectra):
    projected = [jnp.dot(tokens, projection_weights[which], preferred_element_type=jnp.float32).astype(jnp.bfloat16) for which in range(3)]
    filtered = [short_filter(projected[which].astype(jnp.float32), short_taps[which]) for which in range(3)]
    gated = filtered[1] * filtered[2]
    length = gated.shape[0]
    channels = gated.shape[1]
    block = min(channels, 1024)
    pieces = []
    for start in range(0, channels, block):
        segment = gated[:, start:start + block]
        padded = jnp.concatenate([segment, jnp.zeros_like(segment)], axis=0)
        spectrum = jnp.fft.fft(padded, axis=0)
        product = lax.complex(filter_spectra[0, :, start:start + block], filter_spectra[1, :, start:start + block]) * spectrum
        pieces.append(jnp.real(jnp.fft.ifft(product, axis=0))[:length])
    long_conv = jnp.concatenate(pieces, axis=1)
    return (filtered[0] * long_conv).astype(jnp.bfloat16)
```

```python
import numpy as np

import jax
import jax.numpy as jnp
from jax import lax
from jax.experimental import pallas as pl
from jax.experimental.pallas import tpu as pltpu
from jax.sharding import PartitionSpec as P


SWAP = [(0, 1), (1, 0)]


def project_kernel(core_ref, x_ref, own_ref, other_ref, out_ref):
    core = core_ref[0]
    half, rows, width = x_ref.shape[0] // 2, x_ref.shape[1], x_ref.shape[2]
    count = own_ref.shape[0]
    step = 8
    total = None
    for first, weights in ((core * half, own_ref), ((1 - core) * half, other_ref)):
        for start in range(0, half, step):
            x = jnp.concatenate([x_ref[first + start + i] for i in range(step)], axis=1)
            span = slice(start * width, (start + step) * width)
            w = jnp.concatenate([weights[p, span, :] for p in range(count)], axis=1)
            part = jnp.dot(x, w, preferred_element_type=jnp.float32)
            total = part if total is None else total + part
    for p in range(count):
        out_ref[p] = total[:, p * width : (p + 1) * width].astype(out_ref.dtype)


def split(x):
    high = x.astype(jnp.bfloat16)
    return high, (x - high.astype(jnp.float32)).astype(jnp.bfloat16)


def product(table, data):
    def dot(a, b):
        return jnp.dot(a, b, preferred_element_type=jnp.float32)

    return dot(table[0], data[0]) + (dot(table[0], data[1]) + dot(table[1], data[0]))


def mix_kernel(core_ref, own_ref, other_ref, taps_ref, spec_own_ref, spec_other_ref, table_ref, out_ref):
    first = core_ref[0] == 0
    rows, width = own_ref.shape[1:]
    length = 2 * rows
    taps = taps_ref.shape[1]

    def ordered(a, b):
        return jnp.concatenate([jnp.where(first, a, b), jnp.where(first, b, a)], axis=0)

    def halves(x):
        return jnp.where(first, x[:rows], x[rows:])

    position = lax.broadcasted_iota(jnp.int32, (length, width), 0)

    def filtered(p):
        x = ordered(own_ref[p].astype(jnp.float32), other_ref[p].astype(jnp.float32))
        result = taps_ref[p, 0:1, :] * x
        for j in range(1, taps):
            moved = jnp.where(position < j, 0.0, pltpu.roll(x, j, 0))
            result = result + taps_ref[p, j : j + 1, :] * moved
        return result

    gate = halves(filtered(0))
    gated = filtered(1) * filtered(2)
    sign = (1 - 2 * (position % 2)).astype(jnp.float32)
    data = split(jnp.concatenate([gated, sign * gated], axis=1))
    real = product((table_ref[0], table_ref[1]), data)
    imag = -product((table_ref[2], table_ref[3]), data)

    def spectra(part):
        a, b = spec_own_ref[part], spec_other_ref[part]
        return jnp.concatenate([jnp.where(first, a, b), jnp.where(first, b, a)], axis=1)

    spec_real, spec_imag = spectra(0), spectra(1)
    prod_real = split(spec_real * real - spec_imag * imag)
    prod_imag = split(spec_real * imag + spec_imag * real)
    mine = pl.ds(pl.multiple_of(core_ref[0] * rows, rows), rows)
    cosine = (table_ref[0, mine, :], table_ref[1, mine, :])
    sine = (table_ref[2, mine, :], table_ref[3, mine, :])
    back = product(cosine, prod_real) - product(sine, prod_imag)
    long_conv = (back[:, :width] + sign[:rows] * back[:, width:]) * (1.0 / (2 * length))
    out_ref[...] = (gate * long_conv).astype(out_ref.dtype)


def tables(length):
    index = np.arange(length)
    turn = (index[:, None] * index[None, :]) % (2 * length) * (np.pi / length)
    parts = []
    for exact in (np.cos(turn), np.sin(turn)):
        high = exact.astype(jnp.bfloat16)
        parts += [high, (exact - high.astype(np.float64)).astype(jnp.bfloat16)]
    return np.stack(parts)


def on_chip(kernel, out, *args):
    specs = [pl.BlockSpec(memory_space=pltpu.SMEM)]
    specs += [pl.BlockSpec(memory_space=pltpu.VMEM)] * (len(args) - 1)
    return pl.pallas_call(
        kernel,
        out_shape=out,
        in_specs=specs,
        out_specs=pl.BlockSpec(memory_space=pltpu.VMEM),
    )(*args)


def shards(tokens, projection_weights, short_taps, filter_spectra):
    chips = lax.axis_size("chan")
    rows, width = tokens.shape
    count = projection_weights.shape[0]
    core = lax.axis_index("seq").astype(jnp.int32)[None]
    other_weights = lax.ppermute(projection_weights, "seq", SWAP)
    other_spectra = lax.ppermute(filter_spectra, "seq", SWAP)
    copies = jnp.broadcast_to(tokens[None], (chips, rows, width))
    features = lax.all_to_all(copies, "chan", split_axis=0, concat_axis=0, tiled=True)
    projected = on_chip(
        project_kernel,
        jax.ShapeDtypeStruct((count, rows, width), jnp.bfloat16),
        core,
        features,
        projection_weights,
        other_weights,
    )
    other = lax.ppermute(projected, "seq", SWAP)
    return on_chip(
        mix_kernel,
        jax.ShapeDtypeStruct((rows, width), jnp.bfloat16),
        core,
        projected,
        other,
        short_taps,
        filter_spectra,
        other_spectra,
        jnp.asarray(tables(2 * rows)),
    )


def solution(mesh):
    return jax.shard_map(
        shards,
        mesh=mesh,
        in_specs=(
            P("seq", "chan"),
            P(None, "seq", "chan"),
            P(None, None, "chan"),
            P(None, "seq", "chan"),
        ),
        out_specs=P("seq", "chan"),
        check_vma=False,
    )
```

```python
import numpy as np

import jax
import jax.numpy as jnp
from jax import lax
from jax.experimental import pallas as pl
from jax.experimental.pallas import tpu as pltpu
from jax.sharding import PartitionSpec as P


SWAP = [(0, 1), (1, 0)]
GROUP = 16
MOVES = (
    (1, 0, 12, ((0, 0, 1), (-1, 0, 0))),
    (2, 0, 10, ((0, 1, 0), (0, -1, 0))),
    (3, 0, 9, ((0, 0, -1), (1, 0, 0))),
    (3, 9, 16, ((1, 0, 0), (0, 0, -1))),
    (2, 10, 16, ((0, -1, 0), (0, 1, 0))),
    (1, 12, 16, ((-1, 0, 0), (0, 0, 1))),
)


def project_kernel(place_ref, near_ref, *refs):
    pieces, (own_ref, other_ref, out_ref) = refs[:-3], refs[-3:]
    core, label = place_ref[0], place_ref[1]
    rows, width = near_ref.shape[1:]
    count = own_ref.shape[0]
    half = GROUP // 2
    blocks = {(0, i): near_ref.at[i] for i in range(GROUP)}
    for ref, (step, start, stop, _) in zip(pieces, MOVES):
        for i in range(start, stop):
            blocks[step, i] = ref.at[i - start]
    total = None
    for step in range(4):
        for side, weights in ((0, own_ref), (1, other_ref)):
            x = jnp.concatenate([blocks[step, side * half + i][...] for i in range(half)], axis=1)
            spans = []
            for i in range(half):
                z, y = i // 4, i % 4
                turn = lax.rem(label + step + 2 * (core + side) + z + 2 * y, 4)
                spans.append(pl.ds(pl.multiple_of((i * 4 + turn) * width, width), width))
            w = jnp.concatenate(
                [jnp.concatenate([weights[p, span, :] for span in spans], axis=0) for p in range(count)],
                axis=1,
            )
            part = jnp.dot(x, w, preferred_element_type=jnp.float32)
            total = part if total is None else total + part
    for p in range(count):
        out_ref[p] = total[:, p * width : (p + 1) * width].astype(out_ref.dtype)


def split(x):
    high = x.astype(jnp.bfloat16)
    return high, (x - high.astype(jnp.float32)).astype(jnp.bfloat16)


def product(table, data):
    def dot(a, b):
        return jnp.dot(a, b, preferred_element_type=jnp.float32)

    return dot(table[0], data[0]) + (dot(table[0], data[1]) + dot(table[1], data[0]))


def mix_kernel(core_ref, own_ref, other_ref, taps_ref, spec_own_ref, spec_other_ref, table_ref, out_ref):
    first = core_ref[0] == 0
    rows, width = own_ref.shape[1:]
    length = 2 * rows
    taps = taps_ref.shape[1]

    def ordered(a, b):
        return jnp.concatenate([jnp.where(first, a, b), jnp.where(first, b, a)], axis=0)

    def halves(x):
        return jnp.where(first, x[:rows], x[rows:])

    position = lax.broadcasted_iota(jnp.int32, (length, width), 0)

    def filtered(p):
        x = ordered(own_ref[p].astype(jnp.float32), other_ref[p].astype(jnp.float32))
        result = taps_ref[p, 0:1, :] * x
        for j in range(1, taps):
            moved = jnp.where(position < j, 0.0, pltpu.roll(x, j, 0))
            result = result + taps_ref[p, j : j + 1, :] * moved
        return result

    gate = halves(filtered(0))
    gated = filtered(1) * filtered(2)
    sign = (1 - 2 * (position % 2)).astype(jnp.float32)
    data = split(jnp.concatenate([gated, sign * gated], axis=1))
    real = product((table_ref[0], table_ref[1]), data)
    imag = -product((table_ref[2], table_ref[3]), data)

    def spectra(part):
        a, b = spec_own_ref[part], spec_other_ref[part]
        return jnp.concatenate([jnp.where(first, a, b), jnp.where(first, b, a)], axis=1)

    spec_real, spec_imag = spectra(0), spectra(1)
    prod_real = split(spec_real * real - spec_imag * imag)
    prod_imag = split(spec_real * imag + spec_imag * real)
    mine = pl.ds(pl.multiple_of(core_ref[0] * rows, rows), rows)
    cosine = (table_ref[0, mine, :], table_ref[1, mine, :])
    sine = (table_ref[2, mine, :], table_ref[3, mine, :])
    back = product(cosine, prod_real) - product(sine, prod_imag)
    long_conv = (back[:, :width] + sign[:rows] * back[:, width:]) * (1.0 / (2 * length))
    out_ref[...] = (gate * long_conv).astype(out_ref.dtype)


def tables(length):
    index = np.arange(length)
    turn = (index[:, None] * index[None, :]) % (2 * length) * (np.pi / length)
    parts = []
    for exact in (np.cos(turn), np.sin(turn)):
        high = exact.astype(jnp.bfloat16)
        parts += [high, (exact - high.astype(np.float64)).astype(jnp.bfloat16)]
    return np.stack(parts)


def on_chip(kernel, shape, core, *args):
    specs = [pl.BlockSpec(memory_space=pltpu.SMEM)] * len(core)
    specs += [pl.BlockSpec(memory_space=pltpu.VMEM)] * len(args)
    args = [pltpu.with_memory_space_constraint(arg, pltpu.VMEM) for arg in args]
    return pl.pallas_call(
        kernel,
        out_shape=pltpu.VMEM(shape, jnp.bfloat16),
        in_specs=specs,
        out_specs=pl.BlockSpec(memory_space=pltpu.VMEM),
        compiler_params=pltpu.CompilerParams(vmem_limit_bytes=16 << 20),
    )(*core, *args)


def chip(z, y, x):
    return (z % 4) * 16 + (y % 4) * 4 + x % 4


def label_groups():
    groups = []
    for core in range(2):
        for label in range(4):
            groups.append([])
            for z in (2 * core + k for k in range(4)):
                for y in range(4):
                    groups[-1].append(core * 64 + chip(z, y, label + z + 2 * y))
    return groups


def from_neighbour(x, hops):
    pairs = []
    for core, (dz, dy, dx) in enumerate(hops):
        for z in range(4):
            for y in range(4):
                for x_ in range(4):
                    source = core * 64 + chip(z + dz, y + dy, x_ + dx)
                    pairs.append((source, core * 64 + chip(z, y, x_)))
    return lax.ppermute(x, ("seq", "chan"), pairs)


def shards(tokens, projection_weights, short_taps, filter_spectra):
    rows, width = tokens.shape
    count = projection_weights.shape[0]
    core = lax.axis_index("seq").astype(jnp.int32)
    index = lax.axis_index("chan").astype(jnp.int32)
    label = (index + 2 * (index // 4) + 3 * (index // 16)) % 4
    place = jnp.stack([core, label])
    other_weights = lax.ppermute(projection_weights, "seq", SWAP)
    copies = jnp.broadcast_to(tokens[None], (GROUP, rows, width))
    copies, spectra, taps, place = lax.optimization_barrier(
        (copies, filter_spectra, short_taps, place)
    )
    near = lax.all_to_all(
        copies,
        ("seq", "chan"),
        split_axis=0,
        concat_axis=0,
        axis_index_groups=label_groups(),
        tiled=True,
    )
    near, filter_spectra, short_taps, place = lax.optimization_barrier((near, spectra, taps, place))
    pieces = [from_neighbour(near[start:stop], hops) for _, start, stop, hops in MOVES]
    other_spectra = lax.ppermute(filter_spectra, "seq", SWAP)
    projected = on_chip(
        project_kernel,
        (count, rows, width),
        (place,),
        near,
        *pieces,
        projection_weights,
        other_weights,
    )
    other = lax.ppermute(projected, "seq", SWAP)
    return on_chip(
        mix_kernel,
        (rows, width),
        (place,),
        projected,
        other,
        short_taps,
        filter_spectra,
        other_spectra,
        jnp.asarray(tables(2 * rows)),
    )


def solution(mesh):
    return jax.shard_map(
        shards,
        mesh=mesh,
        in_specs=(
            P("seq", "chan"),
            P(None, "seq", "chan"),
            P(None, None, "chan"),
            P(None, "seq", "chan"),
        ),
        out_specs=P("seq", "chan"),
        check_vma=False,
    )
```

```python
import numpy as np

import jax
import jax.numpy as jnp
from jax import lax
from jax.experimental import pallas as pl
from jax.experimental.pallas import tpu as pltpu
from jax.sharding import PartitionSpec as P


SWAP = [(0, 1), (1, 0)]
GROUP = 16
MOVES = (
    (1, 0, 12, ((0, 0, 1), (-1, 0, 0))),
    (2, 0, 10, ((0, 1, 0), (0, -1, 0))),
    (3, 0, 9, ((0, 0, -1), (1, 0, 0))),
    (3, 9, 16, ((1, 0, 0), (0, 0, -1))),
    (2, 10, 16, ((0, -1, 0), (0, 1, 0))),
    (1, 12, 16, ((-1, 0, 0), (0, 0, 1))),
)


def place():
    core = lax.axis_index("seq")
    index = lax.axis_index("chan")
    return core, (index % 4 + 2 * (index // 4 % 4) + 3 * (index // 16)) % 4


def label_product(blocks, step, side, weights):
    core, label = place()
    count, half, width = weights.shape[0], GROUP // 2, weights.shape[2]
    x = jnp.concatenate([blocks[step, side * half + i][...] for i in range(half)], axis=1)
    spans = []
    for i in range(half):
        z, y = i // 4, i % 4
        turn = (label + step + 2 * (core + side) + z + 2 * y) % 4
        spans.append(pl.ds(pl.multiple_of((i * 4 + turn) * width, width), width))
    w = jnp.concatenate(
        [jnp.concatenate([weights[p, span, :] for span in spans], axis=0) for p in range(count)],
        axis=1,
    )
    return jnp.dot(x, w, preferred_element_type=jnp.float32)


def near_kernel(near_ref, own_ref, other_hbm, sum_ref, other_ref, sem):
    move = pltpu.make_async_copy(other_hbm, other_ref, sem)
    move.start()
    blocks = {(0, i): near_ref.at[i] for i in range(GROUP)}
    sum_ref[...] = label_product(blocks, 0, 0, own_ref)
    move.wait()
    sum_ref[...] += label_product(blocks, 0, 1, other_ref)


def far_kernel(sum_ref, *refs):
    pieces, (own_ref, other_ref, out_ref) = refs[:-3], refs[-3:]
    count, width = own_ref.shape[0], own_ref.shape[2]
    blocks = {}
    for ref, (step, start, stop, _) in zip(pieces, MOVES):
        for i in range(start, stop):
            blocks[step, i] = ref.at[i - start]
    total = sum_ref[...]
    for step in (1, 2, 3):
        for side, weights in ((0, own_ref), (1, other_ref)):
            total = total + label_product(blocks, step, side, weights)
    for p in range(count):
        out_ref[p] = total[:, p * width : (p + 1) * width].astype(out_ref.dtype)


def split(x):
    high = x.astype(jnp.bfloat16)
    return high, (x - high.astype(jnp.float32)).astype(jnp.bfloat16)


def product(table, data):
    def dot(a, b):
        return jnp.dot(a, b, preferred_element_type=jnp.float32)

    return dot(table[0], data[0]) + (dot(table[0], data[1]) + dot(table[1], data[0]))


def mix_kernel(own_ref, other_ref, taps_ref, spec_own_ref, spec_other_ref, table_ref, out_ref):
    core, _ = place()
    first = core == 0
    rows, width = own_ref.shape[1:]
    length = 2 * rows
    taps = taps_ref.shape[1]

    def ordered(a, b):
        return jnp.concatenate([jnp.where(first, a, b), jnp.where(first, b, a)], axis=0)

    def halves(x):
        return jnp.where(first, x[:rows], x[rows:])

    position = lax.broadcasted_iota(jnp.int32, (length, width), 0)

    def filtered(p):
        x = ordered(own_ref[p].astype(jnp.float32), other_ref[p].astype(jnp.float32))
        result = taps_ref[p, 0:1, :] * x
        for j in range(1, taps):
            moved = jnp.where(position < j, 0.0, pltpu.roll(x, j, 0))
            result = result + taps_ref[p, j : j + 1, :] * moved
        return result

    gate = halves(filtered(0))
    gated = filtered(1) * filtered(2)
    sign = (1 - 2 * (position % 2)).astype(jnp.float32)
    data = split(jnp.concatenate([gated, sign * gated], axis=1))
    real = product((table_ref[0], table_ref[1]), data)
    imag = -product((table_ref[2], table_ref[3]), data)

    def spectra(part):
        a, b = spec_own_ref[part], spec_other_ref[part]
        return jnp.concatenate([jnp.where(first, a, b), jnp.where(first, b, a)], axis=1)

    spec_real, spec_imag = spectra(0), spectra(1)
    prod_real = split(spec_real * real - spec_imag * imag)
    prod_imag = split(spec_real * imag + spec_imag * real)
    mine = pl.ds(pl.multiple_of(core * rows, rows), rows)
    cosine = (table_ref[0, mine, :], table_ref[1, mine, :])
    sine = (table_ref[2, mine, :], table_ref[3, mine, :])
    back = product(cosine, prod_real) - product(sine, prod_imag)
    long_conv = (back[:, :width] + sign[:rows] * back[:, width:]) * (1.0 / (2 * length))
    out_ref[...] = (gate * long_conv).astype(out_ref.dtype)


def tables(length):
    index = np.arange(length)
    turn = (index[:, None] * index[None, :]) % (2 * length) * (np.pi / length)
    parts = []
    for exact in (np.cos(turn), np.sin(turn)):
        high = exact.astype(jnp.bfloat16)
        parts += [high, (exact - high.astype(np.float64)).astype(jnp.bfloat16)]
    return np.stack(parts)


def in_vmem(x):
    return pltpu.with_memory_space_constraint(x, pltpu.VMEM)


def on_chip(kernel, outs, args, hbm=(), scratch=()):
    vmem = pl.BlockSpec(memory_space=pltpu.VMEM)
    return pl.pallas_call(
        kernel,
        out_shape=tuple(pltpu.VMEM(*out) for out in outs),
        in_specs=[vmem] * len(args) + [pl.BlockSpec(memory_space=pl.ANY)] * len(hbm),
        out_specs=(vmem,) * len(outs),
        scratch_shapes=scratch,
        compiler_params=pltpu.CompilerParams(vmem_limit_bytes=16 << 20),
    )(*map(in_vmem, args), *hbm)


def chip(z, y, x):
    return (z % 4) * 16 + (y % 4) * 4 + x % 4


def label_groups():
    groups = []
    for core in range(2):
        for label in range(4):
            groups.append([])
            for z in (2 * core + k for k in range(4)):
                for y in range(4):
                    groups[-1].append(core * 64 + chip(z, y, label + z + 2 * y))
    return groups


def from_neighbour(x, hops):
    pairs = []
    for core, (dz, dy, dx) in enumerate(hops):
        for z in range(4):
            for y in range(4):
                for x_ in range(4):
                    source = core * 64 + chip(z + dz, y + dy, x_ + dx)
                    pairs.append((source, core * 64 + chip(z, y, x_)))
    return lax.ppermute(x, ("seq", "chan"), pairs)


def shards(tokens, projection_weights, short_taps, filter_spectra):
    rows, width = tokens.shape
    count = projection_weights.shape[0]
    other_weights = lax.ppermute(projection_weights, "seq", SWAP)
    copies = jnp.broadcast_to(tokens[None], (GROUP, rows, width))
    copies, spectra, taps = lax.optimization_barrier((copies, filter_spectra, short_taps))
    near = lax.all_to_all(
        copies,
        ("seq", "chan"),
        split_axis=0,
        concat_axis=0,
        axis_index_groups=label_groups(),
        tiled=True,
    )
    near, filter_spectra, short_taps = lax.optimization_barrier((near, spectra, taps))
    pieces = [from_neighbour(near[start:stop], hops) for _, start, stop, hops in MOVES]
    other_spectra = lax.ppermute(filter_spectra, "seq", SWAP)
    partial, other_weights = on_chip(
        near_kernel,
        (((rows, count * width), jnp.float32), (other_weights.shape, jnp.bfloat16)),
        (near, projection_weights),
        (other_weights,),
        (pltpu.SemaphoreType.DMA(()),),
    )
    (projected,) = on_chip(
        far_kernel,
        (((count, rows, width), jnp.bfloat16),),
        (partial, *pieces, projection_weights, other_weights),
    )
    other = lax.ppermute(projected, "seq", SWAP)
    (mixed,) = on_chip(
        mix_kernel,
        (((rows, width), jnp.bfloat16),),
        (
            projected,
            other,
            short_taps,
            filter_spectra,
            other_spectra,
            jnp.asarray(tables(2 * rows)),
        ),
    )
    return mixed


def solution(mesh):
    return jax.shard_map(
        shards,
        mesh=mesh,
        in_specs=(
            P("seq", "chan"),
            P(None, "seq", "chan"),
            P(None, None, "chan"),
            P(None, "seq", "chan"),
        ),
        out_specs=P("seq", "chan"),
        check_vma=False,
    )
```

```python
import functools

import numpy as np

import jax
import jax.numpy as jnp
from jax import lax
from jax.experimental import pallas as pl
from jax.experimental.pallas import tpu as pltpu
from jax.sharding import PartitionSpec as P


SWAP = [(0, 1), (1, 0)]
GROUP = 16
MOVES = ((1, 0, 16, ((0, 0, 1), (-1, 0, 0))), (2, 0, 16, ((0, 1, 0), (0, -1, 0))), (3, 0, 16, ((1, 0, 0), (0, 0, -1))))


def place():
    core = lax.axis_index("seq")
    index = lax.axis_index("chan")
    return core, (index % 4 + 2 * (index // 4 % 4) + 3 * (index // 16)) % 4


def label_product(blocks, step, side, weights):
    core, label = place()
    count, half, width = weights.shape[0], GROUP // 2, weights.shape[2]
    x = jnp.concatenate([blocks[step, side * half + i][...] for i in range(half)], axis=1)
    spans = []
    for i in range(half):
        z, y = i // 4, i % 4
        turn = (label + step + 2 * (core + side) + z + 2 * y) % 4
        spans.append(pl.ds(pl.multiple_of((i * 4 + turn) * width, width), width))
    w = jnp.concatenate(
        [jnp.concatenate([weights[p, span, :] for span in spans], axis=0) for p in range(count)],
        axis=1,
    )
    return jnp.dot(x, w, preferred_element_type=jnp.float32)


def near_kernel(near_ref, own_ref, other_hbm, sum_ref, other_ref, sem):
    move = pltpu.make_async_copy(other_hbm, other_ref, sem)
    move.start()
    blocks = {(0, i): near_ref.at[i] for i in range(GROUP)}
    sum_ref[...] = label_product(blocks, 0, 0, own_ref)
    move.wait()
    sum_ref[...] += label_product(blocks, 0, 1, other_ref)


def add_kernel(step, sum_ref, piece_ref, own_ref, other_ref, out_ref):
    blocks = {(step, i): piece_ref.at[i] for i in range(GROUP)}
    total = sum_ref[...]
    for side, weights in ((0, own_ref), (1, other_ref)):
        total = total + label_product(blocks, step, side, weights)
    if len(out_ref.shape) == 2:
        out_ref[...] = total
    else:
        width = out_ref.shape[2]
        for p in range(out_ref.shape[0]):
            out_ref[p] = total[:, p * width : (p + 1) * width].astype(out_ref.dtype)


def split(x):
    high = x.astype(jnp.bfloat16)
    return high, (x - high.astype(jnp.float32)).astype(jnp.bfloat16)


def product(table, data):
    def dot(a, b):
        return jnp.dot(a, b, preferred_element_type=jnp.float32)

    return dot(table[0], data[0]) + (dot(table[0], data[1]) + dot(table[1], data[0]))


def mix_kernel(own_ref, other_ref, taps_ref, spec_own_ref, spec_other_ref, table_ref, out_ref):
    core, _ = place()
    first = core == 0
    rows, width = own_ref.shape[1:]
    length = 2 * rows
    taps = taps_ref.shape[1]

    def ordered(a, b):
        return jnp.concatenate([jnp.where(first, a, b), jnp.where(first, b, a)], axis=0)

    def halves(x):
        return jnp.where(first, x[:rows], x[rows:])

    position = lax.broadcasted_iota(jnp.int32, (length, width), 0)

    def filtered(p):
        x = ordered(own_ref[p].astype(jnp.float32), other_ref[p].astype(jnp.float32))
        result = taps_ref[p, 0:1, :] * x
        for j in range(1, taps):
            moved = jnp.where(position < j, 0.0, pltpu.roll(x, j, 0))
            result = result + taps_ref[p, j : j + 1, :] * moved
        return result

    gate = halves(filtered(0))
    gated = filtered(1) * filtered(2)
    sign = (1 - 2 * (position % 2)).astype(jnp.float32)
    data = split(jnp.concatenate([gated, sign * gated], axis=1))
    real = product((table_ref[0], table_ref[1]), data)
    imag = -product((table_ref[2], table_ref[3]), data)

    def spectra(part):
        a, b = spec_own_ref[part], spec_other_ref[part]
        return jnp.concatenate([jnp.where(first, a, b), jnp.where(first, b, a)], axis=1)

    spec_real, spec_imag = spectra(0), spectra(1)
    prod_real = split(spec_real * real - spec_imag * imag)
    prod_imag = split(spec_real * imag + spec_imag * real)
    mine = pl.ds(pl.multiple_of(core * rows, rows), rows)
    cosine = (table_ref[0, mine, :], table_ref[1, mine, :])
    sine = (table_ref[2, mine, :], table_ref[3, mine, :])
    back = product(cosine, prod_real) - product(sine, prod_imag)
    long_conv = (back[:, :width] + sign[:rows] * back[:, width:]) * (1.0 / (2 * length))
    out_ref[...] = (gate * long_conv).astype(out_ref.dtype)


def tables(length):
    index = np.arange(length)
    turn = (index[:, None] * index[None, :]) % (2 * length) * (np.pi / length)
    parts = []
    for exact in (np.cos(turn), np.sin(turn)):
        high = exact.astype(jnp.bfloat16)
        parts += [high, (exact - high.astype(np.float64)).astype(jnp.bfloat16)]
    return np.stack(parts)


def in_vmem(x):
    return pltpu.with_memory_space_constraint(x, pltpu.VMEM)


def on_chip(kernel, outs, args, hbm=(), scratch=()):
    vmem = pl.BlockSpec(memory_space=pltpu.VMEM)
    return pl.pallas_call(
        kernel,
        out_shape=tuple(pltpu.VMEM(*out) for out in outs),
        in_specs=[vmem] * len(args) + [pl.BlockSpec(memory_space=pl.ANY)] * len(hbm),
        out_specs=(vmem,) * len(outs),
        scratch_shapes=scratch,
        compiler_params=pltpu.CompilerParams(vmem_limit_bytes=16 << 20),
    )(*map(in_vmem, args), *hbm)


def chip(z, y, x):
    return (z % 4) * 16 + (y % 4) * 4 + x % 4


def label_groups():
    groups = []
    for core in range(2):
        for label in range(4):
            groups.append([])
            for z in (2 * core + k for k in range(4)):
                for y in range(4):
                    groups[-1].append(core * 64 + chip(z, y, label + z + 2 * y))
    return groups


def from_neighbour(x, hops):
    pairs = []
    for core, (dz, dy, dx) in enumerate(hops):
        for z in range(4):
            for y in range(4):
                for x_ in range(4):
                    source = core * 64 + chip(z + dz, y + dy, x_ + dx)
                    pairs.append((source, core * 64 + chip(z, y, x_)))
    return lax.ppermute(x, ("seq", "chan"), pairs)


def shards(tokens, projection_weights, short_taps, filter_spectra):
    rows, width = tokens.shape
    count = projection_weights.shape[0]
    other_weights = lax.ppermute(projection_weights, "seq", SWAP)
    copies = jnp.broadcast_to(tokens[None], (GROUP, rows, width))
    copies, spectra, taps = lax.optimization_barrier((copies, filter_spectra, short_taps))
    near = lax.all_to_all(
        copies,
        ("seq", "chan"),
        split_axis=0,
        concat_axis=0,
        axis_index_groups=label_groups(),
        tiled=True,
    )
    near, filter_spectra, short_taps = lax.optimization_barrier((near, spectra, taps))
    pieces = [from_neighbour(near[start:stop], hops) for _, start, stop, hops in MOVES]
    other_spectra = lax.ppermute(filter_spectra, "seq", SWAP)
    partial, other_weights = on_chip(
        near_kernel,
        (((rows, count * width), jnp.float32), (other_weights.shape, jnp.bfloat16)),
        (near, projection_weights),
        (other_weights,),
        (pltpu.SemaphoreType.DMA(()),),
    )
    for k, piece in enumerate(pieces):
        last = k + 1 == len(pieces)
        out = ((count, rows, width), jnp.bfloat16) if last else ((rows, count * width), jnp.float32)
        (partial,) = on_chip(
            functools.partial(add_kernel, MOVES[k][0]),
            (out,),
            (partial, piece, projection_weights, other_weights),
        )
    projected = partial
    other = lax.ppermute(projected, "seq", SWAP)
    (mixed,) = on_chip(
        mix_kernel,
        (((rows, width), jnp.bfloat16),),
        (
            projected,
            other,
            short_taps,
            filter_spectra,
            other_spectra,
            jnp.asarray(tables(2 * rows)),
        ),
    )
    return mixed


def solution(mesh):
    return jax.shard_map(
        shards,
        mesh=mesh,
        in_specs=(
            P("seq", "chan"),
            P(None, "seq", "chan"),
            P(None, None, "chan"),
            P(None, "seq", "chan"),
        ),
        out_specs=P("seq", "chan"),
        check_vma=False,
    )
```

```python
import functools

import numpy as np

import jax
import jax.numpy as jnp
from jax import lax
from jax.experimental import pallas as pl
from jax.experimental.pallas import tpu as pltpu
from jax.sharding import PartitionSpec as P


SWAP = [(0, 1), (1, 0)]
GROUP = 16
MOVES = ((1, 0, 16, ((0, 0, 1), (-1, 0, 0))), (2, 0, 16, ((0, 1, 0), (0, -1, 0))), (3, 0, 16, ((1, 0, 0), (0, 0, -1))))


def place():
    core = lax.axis_index("seq")
    index = lax.axis_index("chan")
    return core, (index % 4 + 2 * (index // 4 % 4) + 3 * (index // 16)) % 4


def row_place(z, i, label, core):
    y = (label + i * (1 + 2 * core)) % 4
    return y, (label + z + 2 * y) % 4


def label_product(blocks, step, side, weights):
    core, label = place()
    count, half, width = weights.shape[0], GROUP // 2, weights.shape[2]
    x = jnp.concatenate([blocks[step, side * half + i][...] for i in range(half)], axis=1)
    spans = []
    for i in range(half):
        y_at, x_at = row_place(2 * (core + side) + i // 4, i, label + step, core)
        spans.append(pl.ds(pl.multiple_of((i // 4 * 16 + y_at * 4 + x_at) * width, width), width))
    w = jnp.concatenate(
        [jnp.concatenate([weights[p, span, :] for span in spans], axis=0) for p in range(count)],
        axis=1,
    )
    return jnp.dot(x, w, preferred_element_type=jnp.float32)


def near_kernel(near_ref, own_ref, other_hbm, sum_ref, other_ref, sem):
    move = pltpu.make_async_copy(other_hbm, other_ref, sem)
    move.start()
    blocks = {(0, i): near_ref.at[i] for i in range(GROUP)}
    sum_ref[...] = label_product(blocks, 0, 0, own_ref)
    move.wait()
    sum_ref[...] += label_product(blocks, 0, 1, other_ref)


def add_kernel(step, sum_ref, piece_ref, own_ref, other_ref, out_ref):
    blocks = {(step, i): piece_ref.at[i] for i in range(GROUP)}
    total = sum_ref[...]
    for side, weights in ((0, own_ref), (1, other_ref)):
        total = total + label_product(blocks, step, side, weights)
    if len(out_ref.shape) == 2:
        out_ref[...] = total
    else:
        width = out_ref.shape[2]
        for p in range(out_ref.shape[0]):
            out_ref[p] = total[:, p * width : (p + 1) * width].astype(out_ref.dtype)


def split(x):
    high = x.astype(jnp.bfloat16)
    return high, (x - high.astype(jnp.float32)).astype(jnp.bfloat16)


def product(table, data):
    def dot(a, b):
        return jnp.dot(a, b, preferred_element_type=jnp.float32)

    return dot(table[0], data[0]) + (dot(table[0], data[1]) + dot(table[1], data[0]))


def mix_kernel(own_ref, other_ref, taps_ref, spec_own_ref, spec_other_ref, table_ref, out_ref):
    core, _ = place()
    first = core == 0
    rows, width = own_ref.shape[1:]
    length = 2 * rows
    taps = taps_ref.shape[1]

    def ordered(a, b):
        return jnp.concatenate([jnp.where(first, a, b), jnp.where(first, b, a)], axis=0)

    def halves(x):
        return jnp.where(first, x[:rows], x[rows:])

    position = lax.broadcasted_iota(jnp.int32, (length, width), 0)

    def filtered(p):
        x = ordered(own_ref[p].astype(jnp.float32), other_ref[p].astype(jnp.float32))
        result = taps_ref[p, 0:1, :] * x
        for j in range(1, taps):
            moved = jnp.where(position < j, 0.0, pltpu.roll(x, j, 0))
            result = result + taps_ref[p, j : j + 1, :] * moved
        return result

    gate = halves(filtered(0))
    gated = filtered(1) * filtered(2)
    sign = (1 - 2 * (position % 2)).astype(jnp.float32)
    data = split(jnp.concatenate([gated, sign * gated], axis=1))
    real = product((table_ref[0], table_ref[1]), data)
    imag = -product((table_ref[2], table_ref[3]), data)

    def spectra(part):
        a, b = spec_own_ref[part], spec_other_ref[part]
        return jnp.concatenate([jnp.where(first, a, b), jnp.where(first, b, a)], axis=1)

    spec_real, spec_imag = spectra(0), spectra(1)
    prod_real = split(spec_real * real - spec_imag * imag)
    prod_imag = split(spec_real * imag + spec_imag * real)
    mine = pl.ds(pl.multiple_of(core * rows, rows), rows)
    cosine = (table_ref[0, mine, :], table_ref[1, mine, :])
    sine = (table_ref[2, mine, :], table_ref[3, mine, :])
    back = product(cosine, prod_real) - product(sine, prod_imag)
    long_conv = (back[:, :width] + sign[:rows] * back[:, width:]) * (1.0 / (2 * length))
    out_ref[...] = (gate * long_conv).astype(out_ref.dtype)


def tables(length):
    index = np.arange(length)
    turn = (index[:, None] * index[None, :]) % (2 * length) * (np.pi / length)
    parts = []
    for exact in (np.cos(turn), np.sin(turn)):
        high = exact.astype(jnp.bfloat16)
        parts += [high, (exact - high.astype(np.float64)).astype(jnp.bfloat16)]
    return np.stack(parts)


def in_vmem(x):
    return pltpu.with_memory_space_constraint(x, pltpu.VMEM)


def on_chip(kernel, outs, args, hbm=(), scratch=()):
    vmem = pl.BlockSpec(memory_space=pltpu.VMEM)
    return pl.pallas_call(
        kernel,
        out_shape=tuple(pltpu.VMEM(*out) for out in outs),
        in_specs=[vmem] * len(args) + [pl.BlockSpec(memory_space=pl.ANY)] * len(hbm),
        out_specs=(vmem,) * len(outs),
        scratch_shapes=scratch,
        compiler_params=pltpu.CompilerParams(vmem_limit_bytes=16 << 20),
    )(*map(in_vmem, args), *hbm)


def chip(z, y, x):
    return (z % 4) * 16 + (y % 4) * 4 + x % 4


def label_groups():
    groups = []
    for core in range(2):
        for label in range(4):
            groups.append([])
            for i in range(GROUP):
                z = (2 * core + i // 4) % 4
                groups[-1].append(core * 64 + chip(z, *row_place(z, i, label, core)))
    return groups


def from_neighbour(x, hops):
    pairs = []
    for core, (dz, dy, dx) in enumerate(hops):
        for z in range(4):
            for y in range(4):
                for x_ in range(4):
                    source = core * 64 + chip(z + dz, y + dy, x_ + dx)
                    pairs.append((source, core * 64 + chip(z, y, x_)))
    return lax.ppermute(x, ("seq", "chan"), pairs)


def shards(tokens, projection_weights, short_taps, filter_spectra):
    rows, width = tokens.shape
    count = projection_weights.shape[0]
    other_weights = lax.ppermute(projection_weights, "seq", SWAP)
    copies = jnp.broadcast_to(tokens[None], (GROUP, rows, width))
    copies, spectra, taps = lax.optimization_barrier((copies, filter_spectra, short_taps))
    near = lax.all_to_all(
        copies,
        ("seq", "chan"),
        split_axis=0,
        concat_axis=0,
        axis_index_groups=label_groups(),
        tiled=True,
    )
    near, filter_spectra, short_taps = lax.optimization_barrier((near, spectra, taps))
    pieces = [from_neighbour(near[start:stop], hops) for _, start, stop, hops in MOVES]
    other_spectra = lax.ppermute(filter_spectra, "seq", SWAP)
    partial, other_weights = on_chip(
        near_kernel,
        (((rows, count * width), jnp.float32), (other_weights.shape, jnp.bfloat16)),
        (near, projection_weights),
        (other_weights,),
        (pltpu.SemaphoreType.DMA(()),),
    )
    for k, piece in enumerate(pieces):
        last = k + 1 == len(pieces)
        out = ((count, rows, width), jnp.bfloat16) if last else ((rows, count * width), jnp.float32)
        (partial,) = on_chip(
            functools.partial(add_kernel, MOVES[k][0]),
            (out,),
            (partial, piece, projection_weights, other_weights),
        )
    projected = partial
    other = lax.ppermute(projected, "seq", SWAP)
    (mixed,) = on_chip(
        mix_kernel,
        (((rows, width), jnp.bfloat16),),
        (
            projected,
            other,
            short_taps,
            filter_spectra,
            other_spectra,
            jnp.asarray(tables(2 * rows)),
        ),
    )
    return mixed


def solution(mesh):
    return jax.shard_map(
        shards,
        mesh=mesh,
        in_specs=(
            P("seq", "chan"),
            P(None, "seq", "chan"),
            P(None, None, "chan"),
            P(None, "seq", "chan"),
        ),
        out_specs=P("seq", "chan"),
        check_vma=False,
    )
```

```python
import functools

import numpy as np

import jax
import jax.numpy as jnp
from jax import lax
from jax.experimental import pallas as pl
from jax.experimental.pallas import tpu as pltpu
from jax.sharding import PartitionSpec as P


SWAP = [(0, 1), (1, 0)]
GROUP = 16
MOVES = ((1, 0, 16, 2), (2, 0, 16, 1), (3, 0, 16, 0))


def place():
    core = lax.axis_index("seq")
    index = lax.axis_index("chan")
    z, y, x = index // 16, index // 4 % 4, index % 4
    return core, (x + z) % 2 + 2 * ((y + z) % 2)


def row_place(i, label):
    y = i // 2 % 2 * 2 + (label // 2 + i // 4) % 2
    return y, i % 2 * 2 + (label + i // 4) % 2


def label_product(blocks, step, side, weights):
    _, label = place()
    count, half, width = weights.shape[0], GROUP // 2, weights.shape[2]
    x = jnp.concatenate([blocks[step, side * half + i][...] for i in range(half)], axis=1)
    spans = []
    for i in range(half):
        y_at, x_at = row_place(i, label ^ step)
        spans.append(pl.ds(pl.multiple_of((i // 4 * 16 + y_at * 4 + x_at) * width, width), width))
    w = jnp.concatenate(
        [jnp.concatenate([weights[p, span, :] for span in spans], axis=0) for p in range(count)],
        axis=1,
    )
    return jnp.dot(x, w, preferred_element_type=jnp.float32)


def near_kernel(near_ref, own_ref, other_hbm, sum_ref, other_ref, sem):
    move = pltpu.make_async_copy(other_hbm, other_ref, sem)
    move.start()
    blocks = {(0, i): near_ref.at[i] for i in range(GROUP)}
    sum_ref[...] = label_product(blocks, 0, 0, own_ref)
    move.wait()
    sum_ref[...] += label_product(blocks, 0, 1, other_ref)


def add_kernel(step, sum_ref, piece_ref, own_ref, other_ref, out_ref):
    blocks = {(step, i): piece_ref.at[i] for i in range(GROUP)}
    total = sum_ref[...]
    for side, weights in ((0, own_ref), (1, other_ref)):
        total = total + label_product(blocks, step, side, weights)
    if len(out_ref.shape) == 2:
        out_ref[...] = total
    else:
        width = out_ref.shape[2]
        for p in range(out_ref.shape[0]):
            out_ref[p] = total[:, p * width : (p + 1) * width].astype(out_ref.dtype)


def split(x):
    high = x.astype(jnp.bfloat16)
    return high, (x - high.astype(jnp.float32)).astype(jnp.bfloat16)


def product(table, data):
    def dot(a, b):
        return jnp.dot(a, b, preferred_element_type=jnp.float32)

    return dot(table[0], data[0]) + (dot(table[0], data[1]) + dot(table[1], data[0]))


def mix_kernel(own_ref, other_ref, taps_ref, spec_own_ref, spec_other_ref, table_ref, out_ref):
    core, _ = place()
    first = core == 0
    rows, width = own_ref.shape[1:]
    length = 2 * rows
    taps = taps_ref.shape[1]

    def ordered(a, b):
        return jnp.concatenate([jnp.where(first, a, b), jnp.where(first, b, a)], axis=0)

    def halves(x):
        return jnp.where(first, x[:rows], x[rows:])

    position = lax.broadcasted_iota(jnp.int32, (length, width), 0)

    def filtered(p):
        x = ordered(own_ref[p].astype(jnp.float32), other_ref[p].astype(jnp.float32))
        result = taps_ref[p, 0:1, :] * x
        for j in range(1, taps):
            moved = jnp.where(position < j, 0.0, pltpu.roll(x, j, 0))
            result = result + taps_ref[p, j : j + 1, :] * moved
        return result

    gate = halves(filtered(0))
    gated = filtered(1) * filtered(2)
    sign = (1 - 2 * (position % 2)).astype(jnp.float32)
    data = split(jnp.concatenate([gated, sign * gated], axis=1))
    real = product((table_ref[0], table_ref[1]), data)
    imag = -product((table_ref[2], table_ref[3]), data)

    def spectra(part):
        a, b = spec_own_ref[part], spec_other_ref[part]
        return jnp.concatenate([jnp.where(first, a, b), jnp.where(first, b, a)], axis=1)

    spec_real, spec_imag = spectra(0), spectra(1)
    prod_real = split(spec_real * real - spec_imag * imag)
    prod_imag = split(spec_real * imag + spec_imag * real)
    mine = pl.ds(pl.multiple_of(core * rows, rows), rows)
    cosine = (table_ref[0, mine, :], table_ref[1, mine, :])
    sine = (table_ref[2, mine, :], table_ref[3, mine, :])
    back = product(cosine, prod_real) - product(sine, prod_imag)
    long_conv = (back[:, :width] + sign[:rows] * back[:, width:]) * (1.0 / (2 * length))
    out_ref[...] = (gate * long_conv).astype(out_ref.dtype)


def tables(length):
    index = np.arange(length)
    turn = (index[:, None] * index[None, :]) % (2 * length) * (np.pi / length)
    parts = []
    for exact in (np.cos(turn), np.sin(turn)):
        high = exact.astype(jnp.bfloat16)
        parts += [high, (exact - high.astype(np.float64)).astype(jnp.bfloat16)]
    return np.stack(parts)


def in_vmem(x):
    return pltpu.with_memory_space_constraint(x, pltpu.VMEM)


def on_chip(kernel, outs, args, hbm=(), scratch=()):
    vmem = pl.BlockSpec(memory_space=pltpu.VMEM)
    return pl.pallas_call(
        kernel,
        out_shape=tuple(pltpu.VMEM(*out) for out in outs),
        in_specs=[vmem] * len(args) + [pl.BlockSpec(memory_space=pl.ANY)] * len(hbm),
        out_specs=(vmem,) * len(outs),
        scratch_shapes=scratch,
        compiler_params=pltpu.CompilerParams(vmem_limit_bytes=16 << 20),
    )(*map(in_vmem, args), *hbm)


def chip(z, y, x):
    return (z % 4) * 16 + (y % 4) * 4 + x % 4


def label_groups():
    groups = []
    for core in range(2):
        for label in range(4):
            groups.append([])
            for i in range(GROUP):
                groups[-1].append(core * 64 + chip(2 * core + i // 4, *row_place(i, label)))
    return groups


def from_neighbour(block, axis):
    pairs = []
    for core in range(2):
        for z in range(4):
            for y in range(4):
                for x in range(4):
                    peer = [z, y, x]
                    peer[axis] += 1 - 2 * ((peer[axis] + core) % 2)
                    pairs.append((core * 64 + chip(*peer), core * 64 + chip(z, y, x)))
    return lax.ppermute(block, ("seq", "chan"), pairs)


def shards(tokens, projection_weights, short_taps, filter_spectra):
    rows, width = tokens.shape
    count = projection_weights.shape[0]
    other_weights = lax.ppermute(projection_weights, "seq", SWAP)
    copies = jnp.broadcast_to(tokens[None], (GROUP, rows, width))
    copies, spectra, taps = lax.optimization_barrier((copies, filter_spectra, short_taps))
    near = lax.all_to_all(
        copies,
        ("seq", "chan"),
        split_axis=0,
        concat_axis=0,
        axis_index_groups=label_groups(),
        tiled=True,
    )
    near, filter_spectra, short_taps = lax.optimization_barrier((near, spectra, taps))
    pieces = [from_neighbour(near[start:stop], axis) for _, start, stop, axis in MOVES]
    other_spectra = lax.ppermute(filter_spectra, "seq", SWAP)
    partial, other_weights = on_chip(
        near_kernel,
        (((rows, count * width), jnp.float32), (other_weights.shape, jnp.bfloat16)),
        (near, projection_weights),
        (other_weights,),
        (pltpu.SemaphoreType.DMA(()),),
    )
    for k, piece in enumerate(pieces):
        last = k + 1 == len(pieces)
        out = ((count, rows, width), jnp.bfloat16) if last else ((rows, count * width), jnp.float32)
        (partial,) = on_chip(
            functools.partial(add_kernel, MOVES[k][0]),
            (out,),
            (partial, piece, projection_weights, other_weights),
        )
    projected = partial
    other = lax.ppermute(projected, "seq", SWAP)
    (mixed,) = on_chip(
        mix_kernel,
        (((rows, width), jnp.bfloat16),),
        (
            projected,
            other,
            short_taps,
            filter_spectra,
            other_spectra,
            jnp.asarray(tables(2 * rows)),
        ),
    )
    return mixed


def solution(mesh):
    return jax.shard_map(
        shards,
        mesh=mesh,
        in_specs=(
            P("seq", "chan"),
            P(None, "seq", "chan"),
            P(None, None, "chan"),
            P(None, "seq", "chan"),
        ),
        out_specs=P("seq", "chan"),
        check_vma=False,
    )
```

```python
import functools

import numpy as np

import jax
import jax.numpy as jnp
from jax import lax
from jax.experimental import pallas as pl
from jax.experimental.pallas import tpu as pltpu
from jax.sharding import PartitionSpec as P


SWAP = [(0, 1), (1, 0)]
GROUP = 16
MOVES = ((1, 0, 16, 2), (2, 0, 16, 1), (3, 0, 16, 0))


def place():
    core = lax.axis_index("seq")
    index = lax.axis_index("chan")
    z, y, x = index // 16, index // 4 % 4, index % 4
    return core, (x + z) % 2 + 2 * ((y + z) % 2)


def row_place(i, label, core):
    y = (i // 2 % 2 ^ core) * 2 + (label // 2 + i // 4) % 2
    return y, (i % 2 ^ core) * 2 + (label + i // 4) % 2


def label_product(blocks, step, side, weights):
    core, label = place()
    count, half, width = weights.shape[0], GROUP // 2, weights.shape[2]
    x = jnp.concatenate([blocks[step, side * half + i][...] for i in range(half)], axis=1)
    spans = []
    for i in range(half):
        y_at, x_at = row_place(i, label ^ step, core)
        spans.append(pl.ds(pl.multiple_of((i // 4 * 16 + y_at * 4 + x_at) * width, width), width))
    w = jnp.concatenate(
        [jnp.concatenate([weights[p, span, :] for span in spans], axis=0) for p in range(count)],
        axis=1,
    )
    return jnp.dot(x, w, preferred_element_type=jnp.float32)


def near_kernel(near_ref, own_ref, other_hbm, sum_ref, other_ref, sem):
    move = pltpu.make_async_copy(other_hbm, other_ref, sem)
    move.start()
    blocks = {(0, i): near_ref.at[i] for i in range(GROUP)}
    sum_ref[...] = label_product(blocks, 0, 0, own_ref)
    move.wait()
    sum_ref[...] += label_product(blocks, 0, 1, other_ref)


def add_kernel(step, sum_ref, piece_ref, own_ref, other_ref, out_ref):
    blocks = {(step, i): piece_ref.at[i] for i in range(GROUP)}
    total = sum_ref[...]
    for side, weights in ((0, own_ref), (1, other_ref)):
        total = total + label_product(blocks, step, side, weights)
    if len(out_ref.shape) == 2:
        out_ref[...] = total
    else:
        width = out_ref.shape[2]
        for p in range(out_ref.shape[0]):
            out_ref[p] = total[:, p * width : (p + 1) * width].astype(out_ref.dtype)


def split(x):
    high = x.astype(jnp.bfloat16)
    return high, (x - high.astype(jnp.float32)).astype(jnp.bfloat16)


def product(table, data):
    def dot(a, b):
        return jnp.dot(a, b, preferred_element_type=jnp.float32)

    return dot(table[0], data[0]) + (dot(table[0], data[1]) + dot(table[1], data[0]))


def mix_kernel(own_ref, other_ref, taps_ref, spec_own_ref, spec_other_ref, table_ref, out_ref):
    core, _ = place()
    first = core == 0
    rows, width = own_ref.shape[1:]
    length = 2 * rows
    taps = taps_ref.shape[1]

    def ordered(a, b):
        return jnp.concatenate([jnp.where(first, a, b), jnp.where(first, b, a)], axis=0)

    def halves(x):
        return jnp.where(first, x[:rows], x[rows:])

    position = lax.broadcasted_iota(jnp.int32, (length, width), 0)

    def filtered(p):
        x = ordered(own_ref[p].astype(jnp.float32), other_ref[p].astype(jnp.float32))
        result = taps_ref[p, 0:1, :] * x
        for j in range(1, taps):
            moved = jnp.where(position < j, 0.0, pltpu.roll(x, j, 0))
            result = result + taps_ref[p, j : j + 1, :] * moved
        return result

    gate = halves(filtered(0))
    gated = filtered(1) * filtered(2)
    sign = (1 - 2 * (position % 2)).astype(jnp.float32)
    data = split(jnp.concatenate([gated, sign * gated], axis=1))
    real = product((table_ref[0], table_ref[1]), data)
    imag = -product((table_ref[2], table_ref[3]), data)

    def spectra(part):
        a, b = spec_own_ref[part], spec_other_ref[part]
        return jnp.concatenate([jnp.where(first, a, b), jnp.where(first, b, a)], axis=1)

    spec_real, spec_imag = spectra(0), spectra(1)
    prod_real = split(spec_real * real - spec_imag * imag)
    prod_imag = split(spec_real * imag + spec_imag * real)
    mine = pl.ds(pl.multiple_of(core * rows, rows), rows)
    cosine = (table_ref[0, mine, :], table_ref[1, mine, :])
    sine = (table_ref[2, mine, :], table_ref[3, mine, :])
    back = product(cosine, prod_real) - product(sine, prod_imag)
    long_conv = (back[:, :width] + sign[:rows] * back[:, width:]) * (1.0 / (2 * length))
    out_ref[...] = (gate * long_conv).astype(out_ref.dtype)


def tables(length):
    index = np.arange(length)
    turn = (index[:, None] * index[None, :]) % (2 * length) * (np.pi / length)
    parts = []
    for exact in (np.cos(turn), np.sin(turn)):
        high = exact.astype(jnp.bfloat16)
        parts += [high, (exact - high.astype(np.float64)).astype(jnp.bfloat16)]
    return np.stack(parts)


def in_vmem(x):
    return pltpu.with_memory_space_constraint(x, pltpu.VMEM)


def on_chip(kernel, outs, args, hbm=(), scratch=()):
    vmem = pl.BlockSpec(memory_space=pltpu.VMEM)
    return pl.pallas_call(
        kernel,
        out_shape=tuple(pltpu.VMEM(*out) for out in outs),
        in_specs=[vmem] * len(args) + [pl.BlockSpec(memory_space=pl.ANY)] * len(hbm),
        out_specs=(vmem,) * len(outs),
        scratch_shapes=scratch,
        compiler_params=pltpu.CompilerParams(vmem_limit_bytes=16 << 20),
    )(*map(in_vmem, args), *hbm)


def chip(z, y, x):
    return (z % 4) * 16 + (y % 4) * 4 + x % 4


def label_groups():
    groups = []
    for core in range(2):
        for label in range(4):
            groups.append([])
            for i in range(GROUP):
                groups[-1].append(core * 64 + chip(2 * core + i // 4, *row_place(i, label, core)))
    return groups


def from_neighbour(block, axis):
    pairs = []
    for core in range(2):
        for z in range(4):
            for y in range(4):
                for x in range(4):
                    peer = [z, y, x]
                    peer[axis] += 1 - 2 * ((peer[axis] + core) % 2)
                    pairs.append((core * 64 + chip(*peer), core * 64 + chip(z, y, x)))
    return lax.ppermute(block, ("seq", "chan"), pairs)


def shards(tokens, projection_weights, short_taps, filter_spectra):
    rows, width = tokens.shape
    count = projection_weights.shape[0]
    other_weights = lax.ppermute(projection_weights, "seq", SWAP)
    copies = jnp.broadcast_to(tokens[None], (GROUP, rows, width))
    copies, spectra, taps = lax.optimization_barrier((copies, filter_spectra, short_taps))
    near = lax.all_to_all(
        copies,
        ("seq", "chan"),
        split_axis=0,
        concat_axis=0,
        axis_index_groups=label_groups(),
        tiled=True,
    )
    near, filter_spectra, short_taps = lax.optimization_barrier((near, spectra, taps))
    pieces = [from_neighbour(near[start:stop], axis) for _, start, stop, axis in MOVES]
    other_spectra = lax.ppermute(filter_spectra, "seq", SWAP)
    partial, other_weights = on_chip(
        near_kernel,
        (((rows, count * width), jnp.float32), (other_weights.shape, jnp.bfloat16)),
        (near, projection_weights),
        (other_weights,),
        (pltpu.SemaphoreType.DMA(()),),
    )
    for k, piece in enumerate(pieces):
        last = k + 1 == len(pieces)
        out = ((count, rows, width), jnp.bfloat16) if last else ((rows, count * width), jnp.float32)
        (partial,) = on_chip(
            functools.partial(add_kernel, MOVES[k][0]),
            (out,),
            (partial, piece, projection_weights, other_weights),
        )
    projected = partial
    other = lax.ppermute(projected, "seq", SWAP)
    (mixed,) = on_chip(
        mix_kernel,
        (((rows, width), jnp.bfloat16),),
        (
            projected,
            other,
            short_taps,
            filter_spectra,
            other_spectra,
            jnp.asarray(tables(2 * rows)),
        ),
    )
    return mixed


def solution(mesh):
    return jax.shard_map(
        shards,
        mesh=mesh,
        in_specs=(
            P("seq", "chan"),
            P(None, "seq", "chan"),
            P(None, None, "chan"),
            P(None, "seq", "chan"),
        ),
        out_specs=P("seq", "chan"),
        check_vma=False,
    )
```

```python
import functools

import numpy as np

import jax
import jax.numpy as jnp
from jax import lax
from jax.experimental import pallas as pl
from jax.experimental.pallas import tpu as pltpu
from jax.sharding import PartitionSpec as P


SWAP = [(0, 1), (1, 0)]
GROUP = 16
MOVES = ((3, 0, 16, 0), (2, 0, 16, 1), (1, 0, 16, 2))


def place():
    core = lax.axis_index("seq")
    index = lax.axis_index("chan")
    z, y, x = index // 16, index // 4 % 4, index % 4
    return core, (x + z) % 2 + 2 * ((y + z) % 2)


def row_place(i, label, core):
    y = (i // 2 % 2 ^ core) * 2 + (label // 2 + i // 4) % 2
    return y, (i % 2 ^ core) * 2 + (label + i // 4) % 2


def label_product(blocks, step, side, weights):
    core, label = place()
    count, half, width = weights.shape[0], GROUP // 2, weights.shape[2]
    x = jnp.concatenate([blocks[step, side * half + i][...] for i in range(half)], axis=1)
    spans = []
    for i in range(half):
        y_at, x_at = row_place(i, label ^ step, core)
        spans.append(pl.ds(pl.multiple_of((i // 4 * 16 + y_at * 4 + x_at) * width, width), width))
    w = jnp.concatenate(
        [jnp.concatenate([weights[p, span, :] for span in spans], axis=0) for p in range(count)],
        axis=1,
    )
    return jnp.dot(x, w, preferred_element_type=jnp.float32)


def near_kernel(near_ref, own_ref, other_hbm, sum_ref, other_ref, sem):
    move = pltpu.make_async_copy(other_hbm, other_ref, sem)
    move.start()
    blocks = {(0, i): near_ref.at[i] for i in range(GROUP)}
    sum_ref[...] = label_product(blocks, 0, 0, own_ref)
    move.wait()
    sum_ref[...] += label_product(blocks, 0, 1, other_ref)


def add_kernel(step, sum_ref, piece_ref, own_ref, other_ref, out_ref):
    blocks = {(step, i): piece_ref.at[i] for i in range(GROUP)}
    total = sum_ref[...]
    for side, weights in ((0, own_ref), (1, other_ref)):
        total = total + label_product(blocks, step, side, weights)
    if len(out_ref.shape) == 2:
        out_ref[...] = total
    else:
        width = out_ref.shape[2]
        for p in range(out_ref.shape[0]):
            out_ref[p] = total[:, p * width : (p + 1) * width].astype(out_ref.dtype)


def split(x):
    high = x.astype(jnp.bfloat16)
    return high, (x - high.astype(jnp.float32)).astype(jnp.bfloat16)


def product(table, data):
    def dot(a, b):
        return jnp.dot(a, b, preferred_element_type=jnp.float32)

    return dot(table[0], data[0]) + (dot(table[0], data[1]) + dot(table[1], data[0]))


def mix_kernel(own_ref, other_ref, taps_ref, spec_own_ref, spec_other_ref, table_ref, out_ref):
    core, _ = place()
    first = core == 0
    rows, width = own_ref.shape[1:]
    length = 2 * rows
    taps = taps_ref.shape[1]

    def ordered(a, b):
        return jnp.concatenate([jnp.where(first, a, b), jnp.where(first, b, a)], axis=0)

    def halves(x):
        return jnp.where(first, x[:rows], x[rows:])

    position = lax.broadcasted_iota(jnp.int32, (length, width), 0)

    def filtered(p):
        x = ordered(own_ref[p].astype(jnp.float32), other_ref[p].astype(jnp.float32))
        result = taps_ref[p, 0:1, :] * x
        for j in range(1, taps):
            moved = jnp.where(position < j, 0.0, pltpu.roll(x, j, 0))
            result = result + taps_ref[p, j : j + 1, :] * moved
        return result

    gate = halves(filtered(0))
    gated = filtered(1) * filtered(2)
    sign = (1 - 2 * (position % 2)).astype(jnp.float32)
    data = split(jnp.concatenate([gated, sign * gated], axis=1))
    real = product((table_ref[0], table_ref[1]), data)
    imag = -product((table_ref[2], table_ref[3]), data)

    def spectra(part):
        a, b = spec_own_ref[part], spec_other_ref[part]
        return jnp.concatenate([jnp.where(first, a, b), jnp.where(first, b, a)], axis=1)

    spec_real, spec_imag = spectra(0), spectra(1)
    prod_real = split(spec_real * real - spec_imag * imag)
    prod_imag = split(spec_real * imag + spec_imag * real)
    mine = pl.ds(pl.multiple_of(core * rows, rows), rows)
    cosine = (table_ref[0, mine, :], table_ref[1, mine, :])
    sine = (table_ref[2, mine, :], table_ref[3, mine, :])
    back = product(cosine, prod_real) - product(sine, prod_imag)
    long_conv = (back[:, :width] + sign[:rows] * back[:, width:]) * (1.0 / (2 * length))
    out_ref[...] = (gate * long_conv).astype(out_ref.dtype)


def tables(length):
    index = np.arange(length)
    turn = (index[:, None] * index[None, :]) % (2 * length) * (np.pi / length)
    parts = []
    for exact in (np.cos(turn), np.sin(turn)):
        high = exact.astype(jnp.bfloat16)
        parts += [high, (exact - high.astype(np.float64)).astype(jnp.bfloat16)]
    return np.stack(parts)


def in_vmem(x):
    return pltpu.with_memory_space_constraint(x, pltpu.VMEM)


def on_chip(kernel, outs, args, hbm=(), scratch=()):
    vmem = pl.BlockSpec(memory_space=pltpu.VMEM)
    return pl.pallas_call(
        kernel,
        out_shape=tuple(pltpu.VMEM(*out) for out in outs),
        in_specs=[vmem] * len(args) + [pl.BlockSpec(memory_space=pl.ANY)] * len(hbm),
        out_specs=(vmem,) * len(outs),
        scratch_shapes=scratch,
        compiler_params=pltpu.CompilerParams(vmem_limit_bytes=16 << 20),
    )(*map(in_vmem, args), *hbm)


def chip(z, y, x):
    return (z % 4) * 16 + (y % 4) * 4 + x % 4


def label_groups():
    groups = []
    for core in range(2):
        for label in range(4):
            groups.append([])
            for i in range(GROUP):
                groups[-1].append(core * 64 + chip(2 * core + i // 4, *row_place(i, label, core)))
    return groups


def from_neighbour(block, axis):
    pairs = []
    for core in range(2):
        for z in range(4):
            for y in range(4):
                for x in range(4):
                    peer = [z, y, x]
                    peer[axis] += 1 - 2 * ((peer[axis] + core) % 2)
                    pairs.append((core * 64 + chip(*peer), core * 64 + chip(z, y, x)))
    return lax.ppermute(block, ("seq", "chan"), pairs)


def shards(tokens, projection_weights, short_taps, filter_spectra):
    rows, width = tokens.shape
    count = projection_weights.shape[0]
    other_weights = lax.ppermute(projection_weights, "seq", SWAP)
    copies = jnp.broadcast_to(tokens[None], (GROUP, rows, width))
    copies, spectra, taps = lax.optimization_barrier((copies, filter_spectra, short_taps))
    near = lax.all_to_all(
        copies,
        ("seq", "chan"),
        split_axis=0,
        concat_axis=0,
        axis_index_groups=label_groups(),
        tiled=True,
    )
    near, filter_spectra, short_taps = lax.optimization_barrier((near, spectra, taps))
    pieces = [from_neighbour(near[start:stop], axis) for _, start, stop, axis in MOVES]
    other_spectra = lax.ppermute(filter_spectra, "seq", SWAP)
    partial, other_weights = on_chip(
        near_kernel,
        (((rows, count * width), jnp.float32), (other_weights.shape, jnp.bfloat16)),
        (near, projection_weights),
        (other_weights,),
        (pltpu.SemaphoreType.DMA(()),),
    )
    for k, piece in enumerate(pieces):
        last = k + 1 == len(pieces)
        out = ((count, rows, width), jnp.bfloat16) if last else ((rows, count * width), jnp.float32)
        (partial,) = on_chip(
            functools.partial(add_kernel, MOVES[k][0]),
            (out,),
            (partial, piece, projection_weights, other_weights),
        )
    projected = partial
    other = lax.ppermute(projected, "seq", SWAP)
    (mixed,) = on_chip(
        mix_kernel,
        (((rows, width), jnp.bfloat16),),
        (
            projected,
            other,
            short_taps,
            filter_spectra,
            other_spectra,
            jnp.asarray(tables(2 * rows)),
        ),
    )
    return mixed


def solution(mesh):
    return jax.shard_map(
        shards,
        mesh=mesh,
        in_specs=(
            P("seq", "chan"),
            P(None, "seq", "chan"),
            P(None, None, "chan"),
            P(None, "seq", "chan"),
        ),
        out_specs=P("seq", "chan"),
        check_vma=False,
    )
```

```python
import functools

import numpy as np

import jax
import jax.numpy as jnp
from jax import lax
from jax.experimental import pallas as pl
from jax.experimental.pallas import tpu as pltpu
from jax.sharding import PartitionSpec as P


SWAP = [(0, 1), (1, 0)]
GROUP = 16
MOVES = ((1, 0, 16, 2), (2, 0, 16, 1), (3, 0, 16, 0))


def place():
    core = lax.axis_index("seq")
    index = lax.axis_index("chan")
    z, y, x = index // 16, index // 4 % 4, index % 4
    return core, (x + z) % 2 + 2 * ((y + z) % 2)


def row_place(i, label, core):
    y = i // 2 % 2 * 2 + (label // 2 + i // 4) % 2
    return y, (i % 2 ^ core) * 2 + (label + i // 4) % 2


def label_product(blocks, step, side, weights):
    core, label = place()
    count, half, width = weights.shape[0], GROUP // 2, weights.shape[2]
    x = jnp.concatenate([blocks[step, side * half + i][...] for i in range(half)], axis=1)
    spans = []
    for i in range(half):
        y_at, x_at = row_place(i, label ^ step, core)
        spans.append(pl.ds(pl.multiple_of((i // 4 * 16 + y_at * 4 + x_at) * width, width), width))
    w = jnp.concatenate(
        [jnp.concatenate([weights[p, span, :] for span in spans], axis=0) for p in range(count)],
        axis=1,
    )
    return jnp.dot(x, w, preferred_element_type=jnp.float32)


def near_kernel(near_ref, own_ref, other_hbm, sum_ref, other_ref, sem):
    move = pltpu.make_async_copy(other_hbm, other_ref, sem)
    move.start()
    blocks = {(0, i): near_ref.at[i] for i in range(GROUP)}
    sum_ref[...] = label_product(blocks, 0, 0, own_ref)
    move.wait()
    sum_ref[...] += label_product(blocks, 0, 1, other_ref)


def add_kernel(step, sum_ref, piece_ref, own_ref, other_ref, out_ref):
    blocks = {(step, i): piece_ref.at[i] for i in range(GROUP)}
    total = sum_ref[...]
    for side, weights in ((0, own_ref), (1, other_ref)):
        total = total + label_product(blocks, step, side, weights)
    if len(out_ref.shape) == 2:
        out_ref[...] = total
    else:
        width = out_ref.shape[2]
        for p in range(out_ref.shape[0]):
            out_ref[p] = total[:, p * width : (p + 1) * width].astype(out_ref.dtype)


def split(x):
    high = x.astype(jnp.bfloat16)
    return high, (x - high.astype(jnp.float32)).astype(jnp.bfloat16)


def product(table, data):
    def dot(a, b):
        return jnp.dot(a, b, preferred_element_type=jnp.float32)

    return dot(table[0], data[0]) + (dot(table[0], data[1]) + dot(table[1], data[0]))


def mix_kernel(own_ref, other_ref, taps_ref, spec_own_ref, spec_other_ref, table_ref, out_ref):
    core, _ = place()
    first = core == 0
    rows, width = own_ref.shape[1:]
    length = 2 * rows
    taps = taps_ref.shape[1]

    def ordered(a, b):
        return jnp.concatenate([jnp.where(first, a, b), jnp.where(first, b, a)], axis=0)

    def halves(x):
        return jnp.where(first, x[:rows], x[rows:])

    position = lax.broadcasted_iota(jnp.int32, (length, width), 0)

    def filtered(p):
        x = ordered(own_ref[p].astype(jnp.float32), other_ref[p].astype(jnp.float32))
        result = taps_ref[p, 0:1, :] * x
        for j in range(1, taps):
            moved = jnp.where(position < j, 0.0, pltpu.roll(x, j, 0))
            result = result + taps_ref[p, j : j + 1, :] * moved
        return result

    gate = halves(filtered(0))
    gated = filtered(1) * filtered(2)
    sign = (1 - 2 * (position % 2)).astype(jnp.float32)
    data = split(jnp.concatenate([gated, sign * gated], axis=1))
    real = product((table_ref[0], table_ref[1]), data)
    imag = -product((table_ref[2], table_ref[3]), data)

    def spectra(part):
        a, b = spec_own_ref[part], spec_other_ref[part]
        return jnp.concatenate([jnp.where(first, a, b), jnp.where(first, b, a)], axis=1)

    spec_real, spec_imag = spectra(0), spectra(1)
    prod_real = split(spec_real * real - spec_imag * imag)
    prod_imag = split(spec_real * imag + spec_imag * real)
    mine = pl.ds(pl.multiple_of(core * rows, rows), rows)
    cosine = (table_ref[0, mine, :], table_ref[1, mine, :])
    sine = (table_ref[2, mine, :], table_ref[3, mine, :])
    back = product(cosine, prod_real) - product(sine, prod_imag)
    long_conv = (back[:, :width] + sign[:rows] * back[:, width:]) * (1.0 / (2 * length))
    out_ref[...] = (gate * long_conv).astype(out_ref.dtype)


def tables(length):
    index = np.arange(length)
    turn = (index[:, None] * index[None, :]) % (2 * length) * (np.pi / length)
    parts = []
    for exact in (np.cos(turn), np.sin(turn)):
        high = exact.astype(jnp.bfloat16)
        parts += [high, (exact - high.astype(np.float64)).astype(jnp.bfloat16)]
    return np.stack(parts)


def in_vmem(x):
    return pltpu.with_memory_space_constraint(x, pltpu.VMEM)


def on_chip(kernel, outs, args, hbm=(), scratch=()):
    vmem = pl.BlockSpec(memory_space=pltpu.VMEM)
    return pl.pallas_call(
        kernel,
        out_shape=tuple(pltpu.VMEM(*out) for out in outs),
        in_specs=[vmem] * len(args) + [pl.BlockSpec(memory_space=pl.ANY)] * len(hbm),
        out_specs=(vmem,) * len(outs),
        scratch_shapes=scratch,
        compiler_params=pltpu.CompilerParams(vmem_limit_bytes=16 << 20),
    )(*map(in_vmem, args), *hbm)


def chip(z, y, x):
    return (z % 4) * 16 + (y % 4) * 4 + x % 4


def label_groups():
    groups = []
    for core in range(2):
        for label in range(4):
            groups.append([])
            for i in range(GROUP):
                groups[-1].append(core * 64 + chip(2 * core + i // 4, *row_place(i, label, core)))
    return groups


def from_neighbour(block, axis):
    pairs = []
    for core in range(2):
        for z in range(4):
            for y in range(4):
                for x in range(4):
                    peer = [z, y, x]
                    peer[axis] += 1 - 2 * ((peer[axis] + core) % 2)
                    pairs.append((core * 64 + chip(*peer), core * 64 + chip(z, y, x)))
    return lax.ppermute(block, ("seq", "chan"), pairs)


def shards(tokens, projection_weights, short_taps, filter_spectra):
    rows, width = tokens.shape
    count = projection_weights.shape[0]
    other_weights = lax.ppermute(projection_weights, "seq", SWAP)
    copies = jnp.broadcast_to(tokens[None], (GROUP, rows, width))
    copies, spectra, taps = lax.optimization_barrier((copies, filter_spectra, short_taps))
    near = lax.all_to_all(
        copies,
        ("seq", "chan"),
        split_axis=0,
        concat_axis=0,
        axis_index_groups=label_groups(),
        tiled=True,
    )
    near, filter_spectra, short_taps = lax.optimization_barrier((near, spectra, taps))
    pieces = [from_neighbour(near[start:stop], axis) for _, start, stop, axis in MOVES]
    other_spectra = lax.ppermute(filter_spectra, "seq", SWAP)
    partial, other_weights = on_chip(
        near_kernel,
        (((rows, count * width), jnp.float32), (other_weights.shape, jnp.bfloat16)),
        (near, projection_weights),
        (other_weights,),
        (pltpu.SemaphoreType.DMA(()),),
    )
    for k, piece in enumerate(pieces):
        last = k + 1 == len(pieces)
        out = ((count, rows, width), jnp.bfloat16) if last else ((rows, count * width), jnp.float32)
        (partial,) = on_chip(
            functools.partial(add_kernel, MOVES[k][0]),
            (out,),
            (partial, piece, projection_weights, other_weights),
        )
    projected = partial
    other = lax.ppermute(projected, "seq", SWAP)
    (mixed,) = on_chip(
        mix_kernel,
        (((rows, width), jnp.bfloat16),),
        (
            projected,
            other,
            short_taps,
            filter_spectra,
            other_spectra,
            jnp.asarray(tables(2 * rows)),
        ),
    )
    return mixed


def solution(mesh):
    return jax.shard_map(
        shards,
        mesh=mesh,
        in_specs=(
            P("seq", "chan"),
            P(None, "seq", "chan"),
            P(None, None, "chan"),
            P(None, "seq", "chan"),
        ),
        out_specs=P("seq", "chan"),
        check_vma=False,
    )
```

```python
import functools

import numpy as np

import jax
import jax.numpy as jnp
from jax import lax
from jax.experimental import pallas as pl
from jax.experimental.pallas import tpu as pltpu
from jax.sharding import PartitionSpec as P


SWAP = [(0, 1), (1, 0)]
GROUP = 16
MOVES = ((1, 0, 16, 2), (2, 0, 16, 1), (3, 0, 16, 0))


def place():
    core = lax.axis_index("seq")
    index = lax.axis_index("chan")
    z, y, x = index // 16, index // 4 % 4, index % 4
    return core, (x + z) % 2 + 2 * ((y + z) % 2)


def row_place(i, label, core):
    y = (i // 2 % 2 ^ core) * 2 + (label // 2 + i // 4) % 2
    return y, (i % 2 ^ core) * 2 + (label + i // 4) % 2


def label_product(blocks, step, side, weights):
    core, label = place()
    count, half, width = weights.shape[0], GROUP // 2, weights.shape[2]
    x = jnp.concatenate([blocks[step, side * half + i][...] for i in range(half)], axis=1)
    spans = []
    for i in range(half):
        y_at, x_at = row_place(i, label ^ step, core)
        spans.append(pl.ds(pl.multiple_of((i // 4 * 16 + y_at * 4 + x_at) * width, width), width))
    w = jnp.concatenate(
        [jnp.concatenate([weights[p, span, :] for span in spans], axis=0) for p in range(count)],
        axis=1,
    )
    return jnp.dot(x, w, preferred_element_type=jnp.float32)


def near_kernel(near_ref, own_ref, other_hbm, sum_ref, other_ref, sem):
    move = pltpu.make_async_copy(other_hbm, other_ref, sem)
    move.start()
    blocks = {(0, i): near_ref.at[i] for i in range(GROUP)}
    sum_ref[...] = label_product(blocks, 0, 0, own_ref)
    move.wait()
    sum_ref[...] += label_product(blocks, 0, 1, other_ref)


def add_kernel(step, sum_ref, piece_ref, own_ref, other_ref, out_ref):
    blocks = {(step, i): piece_ref.at[i] for i in range(GROUP)}
    total = sum_ref[...]
    for side, weights in ((0, own_ref), (1, other_ref)):
        total = total + label_product(blocks, step, side, weights)
    if len(out_ref.shape) == 2:
        out_ref[...] = total
    else:
        width = out_ref.shape[2]
        for p in range(out_ref.shape[0]):
            out_ref[p] = total[:, p * width : (p + 1) * width].astype(out_ref.dtype)


def split(x):
    high = x.astype(jnp.bfloat16)
    return high, (x - high.astype(jnp.float32)).astype(jnp.bfloat16)


def product(table, data):
    def dot(a, b):
        return jnp.dot(a, b, preferred_element_type=jnp.float32)

    return dot(table[0], data[0]) + (dot(table[0], data[1]) + dot(table[1], data[0]))


def mix_kernel(own_ref, other_ref, taps_ref, spec_own_ref, spec_other_ref, table_ref, out_ref):
    core, _ = place()
    first = core == 0
    rows, width = own_ref.shape[1:]
    length = 2 * rows
    taps = taps_ref.shape[1]

    def ordered(a, b):
        return jnp.concatenate([jnp.where(first, a, b), jnp.where(first, b, a)], axis=0)

    def halves(x):
        return jnp.where(first, x[:rows], x[rows:])

    position = lax.broadcasted_iota(jnp.int32, (length, width), 0)

    def filtered(p):
        x = ordered(own_ref[p].astype(jnp.float32), other_ref[p].astype(jnp.float32))
        result = taps_ref[p, 0:1, :] * x
        for j in range(1, taps):
            moved = jnp.where(position < j, 0.0, pltpu.roll(x, j, 0))
            result = result + taps_ref[p, j : j + 1, :] * moved
        return result

    gate = halves(filtered(0))
    gated = filtered(1) * filtered(2)
    sign = (1 - 2 * (position % 2)).astype(jnp.float32)
    data = split(jnp.concatenate([gated, sign * gated], axis=1))
    real = product((table_ref[0], table_ref[1]), data)
    imag = -product((table_ref[2], table_ref[3]), data)

    def spectra(part):
        a, b = spec_own_ref[part], spec_other_ref[part]
        return jnp.concatenate([jnp.where(first, a, b), jnp.where(first, b, a)], axis=1)

    spec_real, spec_imag = spectra(0), spectra(1)
    prod_real = split(spec_real * real - spec_imag * imag)
    prod_imag = split(spec_real * imag + spec_imag * real)
    mine = pl.ds(pl.multiple_of(core * rows, rows), rows)
    cosine = (table_ref[0, mine, :], table_ref[1, mine, :])
    sine = (table_ref[2, mine, :], table_ref[3, mine, :])
    back = product(cosine, prod_real) - product(sine, prod_imag)
    long_conv = (back[:, :width] + sign[:rows] * back[:, width:]) * (1.0 / (2 * length))
    out_ref[...] = (gate * long_conv).astype(out_ref.dtype)


def tables(length):
    index = np.arange(length)
    turn = (index[:, None] * index[None, :]) % (2 * length) * (np.pi / length)
    parts = []
    for exact in (np.cos(turn), np.sin(turn)):
        high = exact.astype(jnp.bfloat16)
        parts += [high, (exact - high.astype(np.float64)).astype(jnp.bfloat16)]
    return np.stack(parts)


def in_vmem(x):
    return pltpu.with_memory_space_constraint(x, pltpu.VMEM)


def on_chip(kernel, outs, args, hbm=(), scratch=()):
    vmem = pl.BlockSpec(memory_space=pltpu.VMEM)
    return pl.pallas_call(
        kernel,
        out_shape=tuple(pltpu.VMEM(*out) for out in outs),
        in_specs=[vmem] * len(args) + [pl.BlockSpec(memory_space=pl.ANY)] * len(hbm),
        out_specs=(vmem,) * len(outs),
        scratch_shapes=scratch,
        compiler_params=pltpu.CompilerParams(vmem_limit_bytes=16 << 20),
    )(*map(in_vmem, args), *hbm)


def chip(z, y, x):
    return (z % 4) * 16 + (y % 4) * 4 + x % 4


def label_groups():
    groups = []
    for core in range(2):
        for label in range(4):
            groups.append([])
            for i in range(GROUP):
                groups[-1].append(core * 64 + chip(2 * core + i // 4, *row_place(i, label, core)))
    return groups


def from_neighbour(block, axis):
    pairs = []
    for core in range(2):
        for z in range(4):
            for y in range(4):
                for x in range(4):
                    peer = [z, y, x]
                    peer[axis] += 1 - 2 * ((peer[axis] + core) % 2)
                    pairs.append((core * 64 + chip(*peer), core * 64 + chip(z, y, x)))
    return lax.ppermute(block, ("seq", "chan"), pairs)


def shards(tokens, projection_weights, short_taps, filter_spectra):
    rows, width = tokens.shape
    count = projection_weights.shape[0]
    copies = jnp.broadcast_to(tokens[None], (GROUP, rows, width))
    copies, spectra, taps, projection_weights = lax.optimization_barrier(
        (copies, filter_spectra, short_taps, projection_weights)
    )
    other_weights = lax.ppermute(projection_weights, "seq", SWAP)
    near = lax.all_to_all(
        copies,
        ("seq", "chan"),
        split_axis=0,
        concat_axis=0,
        axis_index_groups=label_groups(),
        tiled=True,
    )
    near, filter_spectra, short_taps = lax.optimization_barrier((near, spectra, taps))
    pieces = [from_neighbour(near[start:stop], axis) for _, start, stop, axis in MOVES]
    other_spectra = lax.ppermute(filter_spectra, "seq", SWAP)
    partial, other_weights = on_chip(
        near_kernel,
        (((rows, count * width), jnp.float32), (other_weights.shape, jnp.bfloat16)),
        (near, projection_weights),
        (other_weights,),
        (pltpu.SemaphoreType.DMA(()),),
    )
    for k, piece in enumerate(pieces):
        last = k + 1 == len(pieces)
        out = ((count, rows, width), jnp.bfloat16) if last else ((rows, count * width), jnp.float32)
        (partial,) = on_chip(
            functools.partial(add_kernel, MOVES[k][0]),
            (out,),
            (partial, piece, projection_weights, other_weights),
        )
    projected = partial
    other = lax.ppermute(projected, "seq", SWAP)
    (mixed,) = on_chip(
        mix_kernel,
        (((rows, width), jnp.bfloat16),),
        (
            projected,
            other,
            short_taps,
            filter_spectra,
            other_spectra,
            jnp.asarray(tables(2 * rows)),
        ),
    )
    return mixed


def solution(mesh):
    return jax.shard_map(
        shards,
        mesh=mesh,
        in_specs=(
            P("seq", "chan"),
            P(None, "seq", "chan"),
            P(None, None, "chan"),
            P(None, "seq", "chan"),
        ),
        out_specs=P("seq", "chan"),
        check_vma=False,
    )
```
